128 devices in a mesh: seq: 32 (over x, y, core), head: 4 (over z).
Axes of the slice: x: 4, y: 4, z: 4, core: 2. Of those that a mesh axis runs over, the one named last changes fastest.
Arguments:
- tokens: bfloat16 [32768, 1536], P('seq', 'head'), may hold values from -6 to 6
- norm_gain: float32 [1536], replicated, may hold values from 0.1 to 1.9
- w_qkv: bfloat16 [1536, 4608], P(None, 'head'), may hold values from -0.15625 to 0.15625
- w_out: bfloat16 [1536, 1536], P('head'), may hold values from -0.15625 to 0.15625
- frame_ids: int32 [32, 16], P('seq'), may hold values from 0 to 7, never falling along the last dimension, each value on 1 to 4 neighbouring positions
- slot_gain: float32 [1536], replicated, may hold values from 0.1 to 1.9
- w_key: bfloat16 [1536, 256], replicated, may hold values from -0.15625 to 0.15625
- w_value: bfloat16 [1536, 256], replicated, may hold values from -0.15625 to 0.15625
- w_query: float32 [256, 256], replicated, may hold values from -0.375 to 0.375
- slot_init: float32 [64, 256], replicated, may hold values from -6 to 6
- w_input: float32 [256, 768], replicated, may hold values from -0.375 to 0.375
- w_hidden: float32 [256, 768], replicated, may hold values from -0.375 to 0.375
Outputs:
- mixed: bfloat16 [32768, 1536], P(('seq', 'head'))
- slots: float32 [64, 256], replicated
The draws below stay inside these ranges and needn't reach their ends.
Inputs may be any that keep to these rules, and one draw needn't show every extreme that they name: `frame_ids`: ids never fall along a row; a frame covers 1 to 4 blocks, and in every row some frame covers exactly 4 blocks.
All inputs are finite; a program needn't handle non-finite values.
Results may differ from the reference program's by a relative error of at most 0.008.
Values may be sent and summed in bfloat16 or wider, within the bound.
A program may use at most 64 MiB of HBM per device.

```python
import math
import jax
import jax.numpy as jnp
import numpy as np
from jax import lax

D = 1536
HEADS = 24
HD = 64
SLOTS = 64
SD = 256
ITERS = 3
BLK = 64
TOK_DEV = 1024
BLOCKS_DEV = 16
TOKENS = 32768
N_SEQ = 32


def steps_of(stream_key, dims, shards, smallest, high):
    def one(position, blocks):
        steps = jax.random.uniform(jax.random.fold_in(jax.random.fold_in(stream_key, 6), position), (blocks,), jnp.float32, smallest / len(shards), high / len(shards))
        return jnp.repeat(jnp.exp(steps), dims[position] // blocks).reshape((-1,) + (1,) * (len(dims) - position - 1))

    loudness = one(*shards[0])
    for cut in shards[1:]:
        loudness = loudness * one(*cut)
    return loudness


def profile(amount, total, bound, slope):
    loads = [(1 << 20) // math.isqrt(standing ** slope) + 1 for standing in range(2, amount + 1)]
    rest, holding = total - bound - (amount - 1), [1] * (amount - 1)
    while rest > 0:
        movable = [i for i in range(amount - 1) if holding[i] < bound]
        whole, left = sum([loads[i] for i in movable]), rest
        for i in movable:
            more = min(bound - holding[i], max(1, left * loads[i] // whole), rest)
            holding[i] = holding[i] + more
            rest = rest - more
    return np.array([bound] + holding)


def uneven(own_key, number_of, total, limit, skew):
    if number_of == 2:
        one = jax.random.randint(own_key, (), max(1, total - limit), min(limit, total - 1) + 1)
        return jnp.stack([one, total - one])
    tallies = jnp.asarray(profile(number_of, total, limit, skew), jnp.int32)
    pairs = (number_of - 1) // 2
    giver, receiver = tallies[1:1 + 2 * pairs:2], tallies[2:2 + 2 * pairs:2]
    margin = jnp.minimum(giver - 1, limit - receiver)
    moved = jax.random.randint(jax.random.fold_in(own_key, 1), (pairs,), 0, 1 << 20) % (margin + 1)
    tallies = tallies.at[1:1 + 2 * pairs:2].set(giver - moved).at[2:2 + 2 * pairs:2].set(receiver + moved)
    return tallies[jax.random.permutation(jax.random.fold_in(own_key, 2), number_of)]


def gaussian(stream_key, extent, width, bound, shards=(), kind=jnp.bfloat16):
    level = steps_of(stream_key, extent, shards, -0.22, 0.18) if shards else 1.0
    array = jax.random.normal(stream_key, extent, jnp.float32) * width * level
    return jnp.minimum(jnp.maximum(array, -bound), bound).astype(kind)


def setup_inputs(seed: int = 0) -> dict:
    arg_keys = jax.random.split(jax.random.key(seed), 13)
    return {
        "tokens": gaussian(arg_keys[0], (TOKENS, D), 1.0, 6.0, ((0, 32), (1, 4))),
        "norm_gain": jnp.clip(1.0 + 0.18 * jax.random.normal(arg_keys[1], (D,), jnp.float32), 0.1, 1.9),
        "w_qkv": gaussian(arg_keys[2], (D, 3 * D), D ** -0.5, 0.15625, ((1, 4),)),
        "w_out": gaussian(arg_keys[3], (D, D), D ** -0.5, 0.15625, ((0, 4),)),
        "frame_ids": jax.vmap(lambda own: jnp.searchsorted(jnp.cumsum(uneven(own, BLOCKS_DEV // 2, BLOCKS_DEV, min(4, BLOCKS_DEV // 2 + 1), 0)), jnp.arange(BLOCKS_DEV), side="right"))(jax.random.split(arg_keys[4], N_SEQ)).reshape((N_SEQ, BLOCKS_DEV)).astype(jnp.int32),
        "slot_gain": jnp.clip(1.0 + 0.18 * jax.random.normal(arg_keys[5], (D,), jnp.float32), 0.1, 1.9),
        "w_key": gaussian(arg_keys[6], (D, SD), D ** -0.5, 0.15625),
        "w_value": gaussian(arg_keys[7], (D, SD), D ** -0.5, 0.15625),
        "w_query": gaussian(arg_keys[8], (SD, SD), SD ** -0.5, 0.375, (), jnp.float32),
        "slot_init": gaussian(arg_keys[9], (SLOTS, SD), 1.0, 6.0, (), jnp.float32),
        "w_input": gaussian(arg_keys[10], (SD, 3 * SD), SD ** -0.5, 0.375, (), jnp.float32),
        "w_hidden": gaussian(arg_keys[11], (SD, 3 * SD), SD ** -0.5, 0.375, (), jnp.float32),
    }


def layer_norm(values, gain):
    mean = lax.optimization_barrier(jnp.mean(values, axis=-1, keepdims=True))
    centred = values - mean
    var = lax.optimization_barrier(jnp.mean(centred * centred, axis=-1, keepdims=True))
    return centred * lax.rsqrt(var + 1e-06) * gain

def normalize_exp(scores):
    powers = jnp.exp(scores)
    return powers / lax.optimization_barrier(jnp.sum(powers, axis=-1, keepdims=True))

def frame_attend(group):
    qkv_rows, ids = group
    tok_ids = jnp.repeat(ids, BLK)
    same = tok_ids[:, None] == tok_ids[None, :]
    split = qkv_rows.reshape(qkv_rows.shape[0], HEADS, 3, HD)

    def one_head(index):
        query = split[:, index, 0, :]
        key = split[:, index, 1, :]
        value = split[:, index, 2, :]
        scores = jnp.dot(query, key.T, preferred_element_type=jnp.float32) * HD ** (-0.5)
        scores = jnp.where(same, scores, -jnp.inf)
        probs = normalize_exp(scores).astype(jnp.bfloat16)
        return jnp.dot(probs, value, preferred_element_type=jnp.float32).astype(jnp.bfloat16)
    outputs = lax.map(one_head, jnp.arange(HEADS, dtype=jnp.int32))
    return jnp.transpose(outputs, (1, 0, 2)).reshape(qkv_rows.shape[0], HEADS * HD)

def recurrent_cell(update, state, w_input, w_hidden):
    high = lax.Precision.HIGHEST
    from_in = jnp.dot(update, w_input, precision=high)
    from_state = jnp.dot(state, w_hidden, precision=high)
    reset = jax.nn.sigmoid(from_in[:, :SD] + from_state[:, :SD])
    gate = jax.nn.sigmoid(from_in[:, SD:2 * SD] + from_state[:, SD:2 * SD])
    candidate = jnp.tanh(from_in[:, 2 * SD:] + reset * from_state[:, 2 * SD:])
    return (1.0 - gate) * candidate + gate * state

def reference(tokens, norm_gain, w_qkv, w_out, frame_ids, slot_gain, w_key, w_value, w_query, slot_init, w_input, w_hidden):
    normed = layer_norm(tokens.astype(jnp.float32), norm_gain).astype(jnp.bfloat16)
    qkv = jnp.dot(normed, w_qkv, preferred_element_type=jnp.float32).astype(jnp.bfloat16)
    grouped = qkv.reshape(N_SEQ, TOK_DEV, 3 * D)
    attended = lax.map(frame_attend, (grouped, frame_ids)).reshape(TOKENS, D)
    projected = jnp.dot(attended, w_out, preferred_element_type=jnp.float32)
    mixed = (tokens.astype(jnp.float32) + projected).astype(jnp.bfloat16)
    slot_in = layer_norm(mixed.astype(jnp.float32), slot_gain).astype(jnp.bfloat16)
    keys = jnp.dot(slot_in, w_key, preferred_element_type=jnp.float32).astype(jnp.bfloat16)
    values = jnp.dot(slot_in, w_value, preferred_element_type=jnp.float32).astype(jnp.bfloat16)
    slots = slot_init
    ones = jnp.ones((SD,), jnp.float32)
    for step in range(ITERS):
        query = jnp.dot(layer_norm(slots, ones), w_query, precision=lax.Precision.HIGHEST).astype(jnp.bfloat16)
        logits = jnp.dot(keys, query.T, preferred_element_type=jnp.float32) * SD ** (-0.5)
        weights = normalize_exp(logits)
        numer = jnp.einsum('ts,td->sd', weights.astype(jnp.bfloat16).astype(jnp.float32), values.astype(jnp.float32))
        denom = lax.optimization_barrier(jnp.sum(weights, axis=0))
        slots = recurrent_cell(numer / denom[:, None], slots, w_input, w_hidden)
    return (mixed, slots)
```

```python
import functools

import jax
import jax.numpy as jnp
from jax import lax
from jax.experimental import pallas as pl
from jax.experimental.pallas import tpu as pltpu
from jax.sharding import PartitionSpec as P

HD = 64
ITERS = 3
BLK = 64
NX, NY, NC, NZ = 4, 4, 2, 4
NG = NZ * NC
NP = NX * NY
HIGH = lax.Precision.HIGHEST
MESH = pl.DeviceIdType.MESH


def layer_norm(values, gain):
    mean = jnp.mean(values, axis=-1, keepdims=True)
    centred = values - mean
    var = jnp.mean(centred * centred, axis=-1, keepdims=True)
    return centred * lax.rsqrt(var + 1e-06) * gain


def plain_norm(values):
    mean = jnp.mean(values, axis=-1, keepdims=True)
    centred = values - mean
    var = jnp.mean(centred * centred, axis=-1, keepdims=True)
    return centred * lax.rsqrt(var + 1e-06)


def normalize_exp(scores):
    powers = jnp.exp(scores)
    return powers / jnp.sum(powers, axis=-1, keepdims=True)


def where_am_i():
    seq, z = lax.axis_index("seq"), lax.axis_index("head")
    core = lax.rem(seq, NC)
    place = lax.div(seq, NC)
    return seq, z, core, place


def slot_kernel(
    keys_ref, values_ref, init_ref, wq_ref, wi_ref, wh_ref, out_ref,
    part, rs_buf, ar_buf, ag_buf, rs_send, rs_recv, ar_send, ar_recv, ag_send, ag_recv,
):
    seq, z, core, place = where_am_i()
    group = z * NC + core
    width = init_ref.shape[1]
    own = init_ref.shape[0] // NG

    def group_peer(step):
        peer = lax.rem(group + step, NG)
        return peer, (place * NC + lax.rem(peer, NC), lax.div(peer, NC))

    def plane_peer(step):
        peer = lax.rem(place + step, NP)
        return peer, (peer * NC + core, z)

    barrier = pltpu.get_barrier_semaphore()
    for step in range(1, NG):
        pl.semaphore_signal(barrier, inc=1, device_id=group_peer(step)[1], device_id_type=MESH)
    for step in range(1, NP):
        pl.semaphore_signal(barrier, inc=1, device_id=plane_peer(step)[1], device_id_type=MESH)

    start = pl.multiple_of(group * own, own)
    state = init_ref[pl.ds(start, own), :]
    query = jnp.dot(
        plain_norm(init_ref[...]), wq_ref[...], precision=HIGH, preferred_element_type=jnp.float32
    ).astype(jnp.bfloat16)
    pl.semaphore_wait(barrier, NG - 1 + NP - 1)

    sent = []
    for it in range(ITERS):
        logits = lax.dot_general(
            query, keys_ref[...], (((1,), (1,)), ((), ())), preferred_element_type=jnp.float32
        ) * width ** (-0.5)
        powers = jnp.exp(logits)
        weights = powers / jnp.sum(powers, axis=0, keepdims=True)
        part[it, :, :width] = jnp.dot(
            weights.astype(jnp.bfloat16), values_ref[...], preferred_element_type=jnp.float32
        )
        denom = jnp.sum(weights, axis=1, keepdims=True)
        part[it, :, width:] = jnp.broadcast_to(denom, (denom.shape[0], 128))

        def rs_copy(step, peer, device):
            return pltpu.make_async_remote_copy(
                src_ref=part.at[it, pl.ds(pl.multiple_of(peer * own, own), own), :],
                dst_ref=rs_buf.at[it, step],
                send_sem=rs_send.at[it, step],
                recv_sem=rs_recv.at[it, step],
                device_id=device,
                device_id_type=MESH,
            )

        copies = [rs_copy(step, *group_peer(step)) for step in range(1, NG)]
        for copy in copies:
            copy.start()
        sent += copies
        from_state = jnp.dot(state, wh_ref[...], precision=HIGH, preferred_element_type=jnp.float32)
        total = part[it, pl.ds(start, own), :]
        for copy in copies:
            copy.wait_recv()
        for step in range(1, NG):
            total = total + rs_buf[it, step]

        ar_buf[it, place] = total

        def ar_copy(step, device):
            return pltpu.make_async_remote_copy(
                src_ref=ar_buf.at[it, place],
                dst_ref=ar_buf.at[it, place],
                send_sem=ar_send.at[it, step],
                recv_sem=ar_recv.at[it, step],
                device_id=device,
                device_id_type=MESH,
            )

        copies = [ar_copy(step, plane_peer(step)[1]) for step in range(1, NP)]
        for copy in copies:
            copy.start()
        sent += copies
        for copy in copies:
            copy.wait_recv()
        total = ar_buf[it, 0]
        for peer in range(1, NP):
            total = total + ar_buf[it, peer]

        update = total[:, :width] / total[:, width : width + 1]
        from_in = jnp.dot(update, wi_ref[...], precision=HIGH, preferred_element_type=jnp.float32)
        reset = jax.nn.sigmoid(from_in[:, :width] + from_state[:, :width])
        gate = jax.nn.sigmoid(
            from_in[:, width : 2 * width] + from_state[:, width : 2 * width]
        )
        candidate = jnp.tanh(from_in[:, 2 * width :] + reset * from_state[:, 2 * width :])
        state = (1.0 - gate) * candidate + gate * state
        if it < ITERS - 1:
            message = jnp.dot(
                plain_norm(state), wq_ref[...], precision=HIGH, preferred_element_type=jnp.float32
            )
        else:
            message = state
        ag_buf[it, pl.ds(start, own), :] = message

        def ag_copy(step, device):
            return pltpu.make_async_remote_copy(
                src_ref=ag_buf.at[it, pl.ds(start, own), :],
                dst_ref=ag_buf.at[it, pl.ds(start, own), :],
                send_sem=ag_send.at[it, step],
                recv_sem=ag_recv.at[it, step],
                device_id=device,
                device_id_type=MESH,
            )

        copies = [ag_copy(step, group_peer(step)[1]) for step in range(1, NG)]
        for copy in copies:
            copy.start()
        sent += copies
        for copy in copies:
            copy.wait_recv()
        if it < ITERS - 1:
            query = ag_buf[it].astype(jnp.bfloat16)
        else:
            out_ref[...] = ag_buf[it]
    for copy in sent:
        copy.wait_send()


def slot_attention(keys, values, slot_init, w_query, w_input, w_hidden):
    slots, width = slot_init.shape
    own = slots // NG
    vmem = pl.BlockSpec(memory_space=pltpu.VMEM)
    return pl.pallas_call(
        slot_kernel,
        out_shape=jax.ShapeDtypeStruct((slots, width), jnp.float32),
        in_specs=[vmem] * 6,
        out_specs=vmem,
        scratch_shapes=[
            pltpu.VMEM((ITERS, slots, width + 128), jnp.float32),
            pltpu.VMEM((ITERS, NG, own, width + 128), jnp.float32),
            pltpu.VMEM((ITERS, NP, own, width + 128), jnp.float32),
            pltpu.VMEM((ITERS, slots, width), jnp.float32),
            pltpu.SemaphoreType.DMA((ITERS, NG)),
            pltpu.SemaphoreType.DMA((ITERS, NG)),
            pltpu.SemaphoreType.DMA((ITERS, NP)),
            pltpu.SemaphoreType.DMA((ITERS, NP)),
            pltpu.SemaphoreType.DMA((ITERS, NG)),
            pltpu.SemaphoreType.DMA((ITERS, NG)),
        ],
        compiler_params=pltpu.CompilerParams(collective_id=0, has_side_effects=True),
        name="slot_attention",
    )(keys, values, slot_init, w_query, w_input, w_hidden)


def local(
    tokens,
    norm_gain,
    w_qkv,
    w_out,
    frame_ids,
    slot_gain,
    w_key,
    w_value,
    w_query,
    slot_init,
    w_input,
    w_hidden,
):
    whole = lax.all_gather(tokens, "head", axis=1, tiled=True)
    tok_count = whole.shape[0]
    normed = layer_norm(whole.astype(jnp.float32), norm_gain).astype(jnp.bfloat16)
    qkv = jnp.dot(normed, w_qkv, preferred_element_type=jnp.float32).astype(jnp.bfloat16)
    heads_here = w_qkv.shape[1] // (3 * HD)
    split = jnp.transpose(qkv.reshape(tok_count, heads_here, 3, HD), (1, 0, 2, 3))
    tok_ids = jnp.repeat(frame_ids[0], BLK)
    same = tok_ids[:, None] == tok_ids[None, :]

    def one_head(head_qkv):
        scores = jnp.dot(
            head_qkv[:, 0, :], head_qkv[:, 1, :].T, preferred_element_type=jnp.float32
        ) * HD ** (-0.5)
        scores = jnp.where(same, scores, -jnp.inf)
        probs = normalize_exp(scores).astype(jnp.bfloat16)
        return jnp.dot(probs, head_qkv[:, 2, :], preferred_element_type=jnp.float32).astype(
            jnp.bfloat16
        )

    outputs = lax.map(one_head, split)
    attended = jnp.transpose(outputs, (1, 0, 2)).reshape(tok_count, heads_here * HD)
    own_rows = tok_count // lax.axis_size("head")
    own_start = lax.axis_index("head") * own_rows
    own = lax.dynamic_slice_in_dim(whole, own_start, own_rows, 0)
    projected = lax.psum_scatter(
        jnp.dot(attended, w_out, preferred_element_type=jnp.float32).astype(jnp.bfloat16),
        "head",
        scatter_dimension=0,
        tiled=True,
    ).astype(jnp.float32)
    mixed = (own.astype(jnp.float32) + projected).astype(jnp.bfloat16)
    slot_in = layer_norm(mixed.astype(jnp.float32), slot_gain).astype(jnp.bfloat16)
    keys = jnp.dot(slot_in, w_key, preferred_element_type=jnp.float32).astype(jnp.bfloat16)
    values = jnp.dot(slot_in, w_value, preferred_element_type=jnp.float32).astype(jnp.bfloat16)
    slots = slot_attention(keys, values, slot_init, w_query, w_input, w_hidden)
    return (mixed, slots)


def solution(mesh):
    placed = (
        P("seq", "head"),
        P(),
        P(None, "head"),
        P("head", None),
        P("seq", None),
        P(),
        P(),
        P(),
        P(),
        P(),
        P(),
        P(),
    )
    return jax.shard_map(
        local,
        mesh=mesh,
        in_specs=placed,
        out_specs=(P(("seq", "head"), None), P()),
        check_vma=False,
    )
```

```python
import functools

import jax
import jax.numpy as jnp
from jax import lax
from jax.experimental import pallas as pl
from jax.experimental.pallas import tpu as pltpu
from jax.sharding import PartitionSpec as P

HD = 64
ITERS = 3
BLK = 64
NX, NY, NC, NZ = 4, 4, 2, 4
NG = NZ * NC
NP = NX * NY
CHUNKS = 4
REACH = 3 * BLK
LAG = 2
HIGH = lax.Precision.HIGHEST
MESH = pl.DeviceIdType.MESH


def plain_norm(values):
    mean = jnp.mean(values, axis=-1, keepdims=True)
    centred = values - mean
    var = jnp.mean(centred * centred, axis=-1, keepdims=True)
    return centred * lax.rsqrt(var + 1e-06)


def block_kernel(
    tokens_ref, wqkv_ref, wout_ref, ids_ref, ngain_ref, sgain_ref, wk_ref, wv_ref,
    init_ref, wq_ref, wi_ref, wh_ref, mixed_ref, slots_ref,
    whole, wqkv, wfull, qkv, att_out, att_in, keys_buf, values_buf,
    part, rs_buf, ar_buf, ag_buf,
    load_sem, own_sem, tok_send, tok_recv, att_send, att_recv, w_send, w_recv,
    rs_send, rs_recv, ar_send, ar_recv, ag_send, ag_recv,
):
    z = lax.axis_index("head")
    seq = lax.axis_index("seq")
    core = lax.rem(seq, NC)
    place = lax.div(seq, NC)
    px, py = lax.div(place, NY), lax.rem(place, NY)
    group = z * NC + core
    rows, cols = tokens_ref.shape
    width = init_ref.shape[1]
    own = init_ref.shape[0] // NG
    chunk = rows // CHUNKS
    half = chunk // 2
    right, left = lax.rem(z + 1, NZ), lax.rem(z + NZ - 1, NZ)

    def device(x, y, c, zz):
        return ((x * NY + y) * NC + c, zz)

    def group_peer(step):
        peer = lax.rem(group + step, NG)
        return peer, (place * NC + lax.rem(peer, NC), lax.div(peer, NC))

    def plane_peer(step):
        peer = lax.rem(place + step, NP)
        return peer, (peer * NC + core, z)

    def remote(src, dst, send, recv, target):
        return pltpu.make_async_remote_copy(
            src_ref=src, dst_ref=dst, send_sem=send, recv_sem=recv,
            device_id=target, device_id_type=MESH,
        )

    barrier = pltpu.get_barrier_semaphore()
    for step in range(1, NG):
        pl.semaphore_signal(barrier, inc=1, device_id=group_peer(step)[1], device_id_type=MESH)
    for step in range(1, NP):
        pl.semaphore_signal(barrier, inc=1, device_id=plane_peer(step)[1], device_id_type=MESH)

    def col(zz):
        return pl.ds(pl.multiple_of(zz * cols, cols), cols)

    load_tokens = pltpu.make_async_copy(tokens_ref, whole.at[:, col(z)], load_sem.at[0])
    load_qkv = pltpu.make_async_copy(wqkv_ref, wqkv, load_sem.at[1])
    load_out = pltpu.make_async_copy(wout_ref, wfull.at[z], load_sem.at[2])
    load_tokens.start()
    load_qkv.start()
    load_out.start()

    start = pl.multiple_of(group * own, own)
    query = jnp.dot(
        plain_norm(init_ref[...]), wq_ref[...], precision=HIGH, preferred_element_type=jnp.float32
    ).astype(jnp.bfloat16)
    pl.semaphore_wait(barrier, NG - 1 + NP - 1)

    def chunk_rows(c):
        return pl.ds(pl.multiple_of(c * chunk, chunk), chunk)

    def own_copy(c, way):
        return remote(
            tokens_ref.at[chunk_rows(c), :],
            whole.at[chunk_rows(c), col(z)],
            tok_send.at[way, c],
            tok_recv.at[way, c],
            (seq, right if way == 0 else left),
        )

    def forward_copy(c, way):
        part_rows = pl.ds(pl.multiple_of(c * chunk + way * half, half), half)
        source = left if way == 0 else right
        return remote(
            whole.at[part_rows, col(source)],
            whole.at[part_rows, col(source)],
            tok_send.at[2 + way, c],
            tok_recv.at[2 + way, c],
            (seq, right if way == 0 else left),
        )

    share = wfull.shape[3]
    wide = wfull.shape[4] // NY
    my_cols = pl.ds(pl.multiple_of(py * wide, wide), wide)

    def first_copy(dz):
        return remote(
            wout_ref.at[px, core, :, my_cols],
            wfull.at[z, px, core, :, my_cols],
            w_send.at[0, dz],
            w_recv.at[0, dz],
            (seq, lax.rem(z + dz, NZ)),
        )

    def x_peer(d):
        return (lax.rem(px + d, NX) * NY + py) * NC + core, z

    def y_peer(d):
        return (px * NY + lax.rem(py + d, NY)) * NC + core, z

    def plane_copy(stage, dz, d):
        zz = lax.rem(z + dz, NZ)
        index = (dz - 1) * 3 + d - 1
        if stage == 1:
            ref = wfull.at[zz, px, core, :, my_cols]
            target = (
                jnp.where(core == 0, x_peer(d)[0], y_peer(d)[0]),
                z,
            )
            return remote(ref, ref, w_send.at[1, index], w_recv.at[1, index], target)
        if stage == 2:
            ref = wfull.at[zz, :, 0, :, my_cols]
            return remote(ref, ref, w_send.at[2, index], w_recv.at[2, index], y_peer(d))
        ref = wfull.at[zz, px, 1, :, :]
        return remote(ref, ref, w_send.at[2, index], w_recv.at[2, index], x_peer(d))

    def last_copy(dz):
        zz = lax.rem(z + dz, NZ)
        ref = wfull.at[zz, :, core, :, :]
        return remote(
            ref, ref, w_send.at[3, dz], w_recv.at[3, dz], (place * NC + 1 - core, z)
        )

    pairs = [(dz, d) for dz in range(1, NZ) for d in range(1, 4)]

    for way in range(2):
        own_copy(0, way).start()
    for dz in range(1, NZ):
        first_copy(dz).start()
    for way in range(2):
        own_copy(1, way).start()

    heads = cols // HD
    span = chunk + 2 * REACH
    qkv[2 * chunk : span, :] = jnp.zeros((span - 2 * chunk, qkv.shape[1]), jnp.bfloat16)
    load_tokens.wait()
    load_qkv.wait()
    lane_block = lax.broadcasted_iota(jnp.int32, (1, span), 1) // BLK

    def attended_copy(c, pair):
        lanes = pl.ds(pair * 2 * HD, 2 * HD)
        there = pl.ds(pl.multiple_of(z * cols + pair * 2 * HD, 2 * HD), 2 * HD)
        return remote(
            att_out.at[chunk_rows(c), lanes],
            att_in.at[:, there],
            att_send.at[c, pair],
            att_recv.at[z, pair],
            (seq, c),
        )

    def project(c):
        x = whole[chunk_rows(c), :].astype(jnp.float32)
        normed = (plain_norm(x) * ngain_ref[...]).astype(jnp.bfloat16)
        qkv[chunk_rows(c), :] = jnp.dot(
            normed, wqkv[...], preferred_element_type=jnp.float32
        ).astype(jnp.bfloat16)

    def attend(c):
        first = pl.multiple_of(jnp.clip(c * chunk - REACH, 0, rows - span), BLK)
        first_block = first // BLK
        key_ids = jnp.zeros((1, span), jnp.int32)
        for b in range(span // BLK):
            key_ids = jnp.where(lane_block == b, ids_ref[0, first_block + b], key_ids)
        same = [
            key_ids == ids_ref[0, c * (chunk // BLK) + b] for b in range(chunk // BLK)
        ]
        for pair in range(heads // 2):
            outputs = []
            for h in range(2):
                base = (2 * pair + h) * 3 * HD
                q = qkv[chunk_rows(c), base : base + HD]
                k = qkv[pl.ds(first, span), base + HD : base + 2 * HD]
                v = qkv[pl.ds(first, span), base + 2 * HD : base + 3 * HD]
                scores = lax.dot_general(
                    q, k, (((1,), (1,)), ((), ())), preferred_element_type=jnp.float32
                )
                probs = []
                for b in range(chunk // BLK):
                    powers = jnp.where(
                        same[b], jnp.exp(scores[b * BLK : (b + 1) * BLK] * HD ** (-0.5)), 0.0
                    )
                    inverse = 1.0 / jnp.sum(powers, axis=-1, keepdims=True)
                    probs.append((powers * inverse).astype(jnp.bfloat16))
                outputs.append(
                    jnp.dot(
                        jnp.concatenate(probs, axis=0), v, preferred_element_type=jnp.float32
                    ).astype(jnp.bfloat16)
                )
            both = jnp.concatenate(outputs, axis=1)

            @pl.when(c == z)
            def _():
                lanes = pl.ds(pl.multiple_of(z * cols + pair * 2 * HD, 2 * HD), 2 * HD)
                att_in[:, lanes] = both

            @pl.when(c != z)
            def _():
                att_out[chunk_rows(c), pair * 2 * HD : (pair + 1) * 2 * HD] = both
                attended_copy(c, pair).start()

    @pl.loop(0, CHUNKS + LAG)
    def _(c):
        @pl.when(c < CHUNKS)
        def _():
            for way in range(2):
                own_copy(c, way).wait_recv()
            for way in range(2):
                forward_copy(c, way).start()

            @pl.when(c + 2 < CHUNKS)
            def _():
                for way in range(2):
                    own_copy(c + 2, way).start()

        @pl.when(c == 0)
        def _():
            for dz in range(1, NZ):
                first_copy(dz).wait_recv()
            for dz, d in pairs:
                plane_copy(1, dz, d).start()

        @pl.when(c == 1)
        def _():
            for dz, d in pairs:
                plane_copy(1, dz, d).wait_recv()

            @pl.when(core == 0)
            def _():
                for dz, d in pairs:
                    plane_copy(2, dz, d).start()

            @pl.when(core == 1)
            def _():
                for dz, d in pairs:
                    plane_copy(3, dz, d).start()

        @pl.when(c >= LAG)
        def _():
            attend(c - LAG)

        @pl.when(c < CHUNKS)
        def _():
            for way in range(2):
                forward_copy(c, way).wait_recv()
            project(c)

        @pl.when(c == CHUNKS - 1)
        def _():
            @pl.when(core == 0)
            def _():
                for dz, d in pairs:
                    plane_copy(2, dz, d).wait_recv()

            @pl.when(core == 1)
            def _():
                for dz, d in pairs:
                    plane_copy(3, dz, d).wait_recv()

            for dz in range(1, NZ):
                last_copy(dz).start()

    load_out.wait()
    for dz in range(1, NZ):
        last_copy(dz).wait_recv()
    for dz in range(1, NZ):
        source = lax.rem(z + dz, NZ)
        for pair in range(heads // 2):
            lanes = pl.ds(pl.multiple_of(source * cols + pair * 2 * HD, 2 * HD), 2 * HD)
            remote(
                att_in.at[:, lanes], att_in.at[:, lanes], att_send.at[source, pair],
                att_recv.at[source, pair], (seq, source),
            ).wait_recv()

    projected = jnp.dot(
        att_in[...],
        wfull[...].reshape(wfull.shape[4], wfull.shape[4]),
        preferred_element_type=jnp.float32,
    )
    mixed = (whole[chunk_rows(z), :].astype(jnp.float32) + projected).astype(jnp.bfloat16)
    mixed_ref[...] = mixed
    slot_in = (plain_norm(mixed.astype(jnp.float32)) * sgain_ref[...]).astype(jnp.bfloat16)
    keys_buf[...] = jnp.dot(slot_in, wk_ref[...], preferred_element_type=jnp.float32).astype(
        jnp.bfloat16
    )
    values_buf[...] = jnp.dot(slot_in, wv_ref[...], preferred_element_type=jnp.float32).astype(
        jnp.bfloat16
    )

    state = init_ref[pl.ds(start, own), :]
    sent = []
    for it in range(ITERS):
        logits = lax.dot_general(
            query, keys_buf[...], (((1,), (1,)), ((), ())), preferred_element_type=jnp.float32
        ) * width ** (-0.5)
        powers = jnp.exp(logits)
        weights = powers / jnp.sum(powers, axis=0, keepdims=True)
        part[it, :, :width] = jnp.dot(
            weights.astype(jnp.bfloat16), values_buf[...], preferred_element_type=jnp.float32
        )
        denom = jnp.sum(weights, axis=1, keepdims=True)
        part[it, :, width:] = jnp.broadcast_to(denom, (denom.shape[0], 128))

        copies = []
        for step in range(1, NG):
            peer, target = group_peer(step)
            copies.append(
                remote(
                    part.at[it, pl.ds(pl.multiple_of(peer * own, own), own), :],
                    rs_buf.at[it, step],
                    rs_send.at[it, step],
                    rs_recv.at[it, step],
                    target,
                )
            )
        for copy in copies:
            copy.start()
        sent += copies
        from_state = jnp.dot(state, wh_ref[...], precision=HIGH, preferred_element_type=jnp.float32)
        total = part[it, pl.ds(start, own), :]
        for copy in copies:
            copy.wait_recv()
        for step in range(1, NG):
            total = total + rs_buf[it, step]

        ar_buf[it, place] = total
        copies = [
            remote(
                ar_buf.at[it, place],
                ar_buf.at[it, place],
                ar_send.at[it, step],
                ar_recv.at[it, step],
                plane_peer(step)[1],
            )
            for step in range(1, NP)
        ]
        for copy in copies:
            copy.start()
        sent += copies
        for copy in copies:
            copy.wait_recv()
        total = ar_buf[it, 0]
        for peer in range(1, NP):
            total = total + ar_buf[it, peer]

        update = total[:, :width] / total[:, width : width + 1]
        from_in = jnp.dot(update, wi_ref[...], precision=HIGH, preferred_element_type=jnp.float32)
        reset = jax.nn.sigmoid(from_in[:, :width] + from_state[:, :width])
        gate = jax.nn.sigmoid(
            from_in[:, width : 2 * width] + from_state[:, width : 2 * width]
        )
        candidate = jnp.tanh(from_in[:, 2 * width :] + reset * from_state[:, 2 * width :])
        state = (1.0 - gate) * candidate + gate * state
        if it < ITERS - 1:
            message = jnp.dot(
                plain_norm(state), wq_ref[...], precision=HIGH, preferred_element_type=jnp.float32
            )
        else:
            message = state
        ag_buf[it, pl.ds(start, own), :] = message
        copies = [
            remote(
                ag_buf.at[it, pl.ds(start, own), :],
                ag_buf.at[it, pl.ds(start, own), :],
                ag_send.at[it, step],
                ag_recv.at[it, step],
                group_peer(step)[1],
            )
            for step in range(1, NG)
        ]
        for copy in copies:
            copy.start()
        sent += copies
        for copy in copies:
            copy.wait_recv()
        if it < ITERS - 1:
            query = ag_buf[it].astype(jnp.bfloat16)
        else:
            slots_ref[...] = ag_buf[it]

    for copy in sent:
        copy.wait_send()

    @pl.loop(0, CHUNKS)
    def _(c):
        for way in range(2):
            own_copy(c, way).wait_send()
            forward_copy(c, way).wait_send()

        @pl.when(c != z)
        def _():
            for pair in range(heads // 2):
                attended_copy(c, pair).wait_send()

    for dz in range(1, NZ):
        first_copy(dz).wait_send()
        last_copy(dz).wait_send()
    for dz, d in pairs:
        plane_copy(1, dz, d).wait_send()

    @pl.when(core == 0)
    def _():
        for dz, d in pairs:
            plane_copy(2, dz, d).wait_send()

    @pl.when(core == 1)
    def _():
        for dz, d in pairs:
            plane_copy(3, dz, d).wait_send()


def local(
    tokens,
    norm_gain,
    w_qkv,
    w_out,
    frame_ids,
    slot_gain,
    w_key,
    w_value,
    w_query,
    slot_init,
    w_input,
    w_hidden,
):
    rows, cols = tokens.shape
    full = cols * NZ
    slots, width = slot_init.shape
    own = slots // NG
    chunk = rows // CHUNKS
    vmem = pl.BlockSpec(memory_space=pltpu.VMEM)
    hbm = pl.BlockSpec(memory_space=pl.ANY)
    share = cols // (NX * NC)
    dma = pltpu.SemaphoreType.DMA
    return pl.pallas_call(
        block_kernel,
        out_shape=(
            jax.ShapeDtypeStruct((chunk, full), jnp.bfloat16),
            jax.ShapeDtypeStruct((slots, width), jnp.float32),
        ),
        in_specs=[hbm, hbm, hbm, pl.BlockSpec(memory_space=pltpu.SMEM)] + [vmem] * 8,
        out_specs=(vmem, vmem),
        scratch_shapes=[
            pltpu.VMEM((rows, full), jnp.bfloat16),
            pltpu.VMEM(w_qkv.shape, jnp.bfloat16),
            pltpu.VMEM((NZ, NX, NC, share, full), jnp.bfloat16),
            pltpu.VMEM((rows, w_qkv.shape[1]), jnp.bfloat16),
            pltpu.VMEM((rows, cols), jnp.bfloat16),
            pltpu.VMEM((chunk, full), jnp.bfloat16),
            pltpu.VMEM((chunk, width), jnp.bfloat16),
            pltpu.VMEM((chunk, width), jnp.bfloat16),
            pltpu.VMEM((ITERS, slots, width + 128), jnp.float32),
            pltpu.VMEM((ITERS, NG, own, width + 128), jnp.float32),
            pltpu.VMEM((ITERS, NP, own, width + 128), jnp.float32),
            pltpu.VMEM((ITERS, slots, width), jnp.float32),
            dma((3,)),
            dma((1,)),
            dma((4, CHUNKS)),
            dma((4, CHUNKS)),
            dma((CHUNKS, 3)),
            dma((NZ, 3)),
            dma((4, 9)),
            dma((4, 9)),
            dma((ITERS, NG)),
            dma((ITERS, NG)),
            dma((ITERS, NP)),
            dma((ITERS, NP)),
            dma((ITERS, NG)),
            dma((ITERS, NG)),
        ],
        compiler_params=pltpu.CompilerParams(
            collective_id=0, has_side_effects=True, vmem_limit_bytes=60 * 1024 * 1024
        ),
        name="vision_block",
    )(
        tokens,
        w_qkv,
        w_out.reshape(NX, NC, share, full),
        frame_ids,
        norm_gain.reshape(1, full),
        slot_gain.reshape(1, full),
        w_key,
        w_value,
        slot_init,
        w_query,
        w_input,
        w_hidden,
    )


def solution(mesh):
    placed = (
        P("seq", "head"),
        P(),
        P(None, "head"),
        P("head", None),
        P("seq", None),
        P(),
        P(),
        P(),
        P(),
        P(),
        P(),
        P(),
    )
    return jax.shard_map(
        local,
        mesh=mesh,
        in_specs=placed,
        out_specs=(P(("seq", "head"), None), P()),
        check_vma=False,
    )
```

```python
import functools

import jax
import jax.numpy as jnp
from jax import lax
from jax.experimental import pallas as pl
from jax.experimental.pallas import tpu as pltpu
from jax.sharding import PartitionSpec as P

HD = 64
ITERS = 3
BLK = 64
NX, NY, NC, NZ = 4, 4, 2, 4
NG = NZ * NC
NP = NX * NY
CHUNKS = 4
REACH = 3 * BLK
LAG = 2
HIGH = lax.Precision.HIGHEST
MESH = pl.DeviceIdType.MESH


def plain_norm(values):
    mean = jnp.mean(values, axis=-1, keepdims=True)
    centred = values - mean
    var = jnp.mean(centred * centred, axis=-1, keepdims=True)
    return centred * lax.rsqrt(var + 1e-06)


def block_kernel(
    tokens_ref, wqkv_ref, wout_ref, wk_hbm, wv_hbm, wi_hbm, wh_hbm, ids_ref, ngain_ref,
    sgain_ref, init_ref, wq_ref, mixed_ref, slots_ref,
    whole, wqkv, wfull, qkv, att_out, att_in, keys_buf, values_buf,
    part, rs_buf, ar_buf, ag_buf, wk_ref, wv_ref, wi_ref, wh_ref,
    load_sem, own_sem, tok_send, tok_recv, att_send, att_recv, w_send, w_recv,
    rs_send, rs_recv, ar_send, ar_recv, ag_send, ag_recv,
):
    z = lax.axis_index("head")
    seq = lax.axis_index("seq")
    core = lax.rem(seq, NC)
    place = lax.div(seq, NC)
    px, py = lax.div(place, NY), lax.rem(place, NY)
    group = z * NC + core
    rows, cols = tokens_ref.shape
    width = init_ref.shape[1]
    own = init_ref.shape[0] // NG
    chunk = rows // CHUNKS
    half = chunk // 2
    right, left = lax.rem(z + 1, NZ), lax.rem(z + NZ - 1, NZ)

    def device(x, y, c, zz):
        return ((x * NY + y) * NC + c, zz)

    def group_peer(step):
        peer = lax.rem(group + step, NG)
        return peer, (place * NC + lax.rem(peer, NC), lax.div(peer, NC))

    def plane_peer(step):
        peer = lax.rem(place + step, NP)
        return peer, (peer * NC + core, z)

    def remote(src, dst, send, recv, target):
        return pltpu.make_async_remote_copy(
            src_ref=src, dst_ref=dst, send_sem=send, recv_sem=recv,
            device_id=target, device_id_type=MESH,
        )

    barrier = pltpu.get_barrier_semaphore()
    for step in range(1, NG):
        pl.semaphore_signal(barrier, inc=1, device_id=group_peer(step)[1], device_id_type=MESH)
    for step in range(1, NP):
        pl.semaphore_signal(barrier, inc=1, device_id=plane_peer(step)[1], device_id_type=MESH)

    def col(zz):
        return pl.ds(pl.multiple_of(zz * cols, cols), cols)

    load_tokens = pltpu.make_async_copy(tokens_ref, whole.at[:, col(z)], load_sem.at[0])
    load_qkv = pltpu.make_async_copy(wqkv_ref, wqkv, load_sem.at[1])
    load_out = pltpu.make_async_copy(wout_ref, wfull.at[z], load_sem.at[2])
    load_tokens.start()
    load_qkv.start()
    load_out.start()
    late = [
        pltpu.make_async_copy(src, dst, load_sem.at[3 + i])
        for i, (src, dst) in enumerate(
            [(wk_hbm, wk_ref), (wv_hbm, wv_ref), (wi_hbm, wi_ref), (wh_hbm, wh_ref)]
        )
    ]
    for copy in late:
        copy.start()

    start = pl.multiple_of(group * own, own)
    query = jnp.dot(
        plain_norm(init_ref[...]), wq_ref[...], precision=HIGH, preferred_element_type=jnp.float32
    ).astype(jnp.bfloat16)
    pl.semaphore_wait(barrier, NG - 1 + NP - 1)

    def chunk_rows(c):
        return pl.ds(pl.multiple_of(c * chunk, chunk), chunk)

    def own_copy(c, way):
        return remote(
            tokens_ref.at[chunk_rows(c), :],
            whole.at[chunk_rows(c), col(z)],
            tok_send.at[way, c],
            tok_recv.at[way, c],
            (seq, right if way == 0 else left),
        )

    def forward_copy(c, way):
        part_rows = pl.ds(pl.multiple_of(c * chunk + way * half, half), half)
        source = left if way == 0 else right
        return remote(
            whole.at[part_rows, col(source)],
            whole.at[part_rows, col(source)],
            tok_send.at[2 + way, c],
            tok_recv.at[2 + way, c],
            (seq, right if way == 0 else left),
        )

    share = wfull.shape[3]
    wide = wfull.shape[4] // NY
    my_cols = pl.ds(pl.multiple_of(py * wide, wide), wide)

    def first_copy(dz):
        return remote(
            wout_ref.at[px, core, :, my_cols],
            wfull.at[z, px, core, :, my_cols],
            w_send.at[0, dz],
            w_recv.at[0, dz],
            (seq, lax.rem(z + dz, NZ)),
        )

    def x_peer(d):
        return (lax.rem(px + d, NX) * NY + py) * NC + core, z

    def y_peer(d):
        return (px * NY + lax.rem(py + d, NY)) * NC + core, z

    def plane_copy(stage, dz, d):
        zz = lax.rem(z + dz, NZ)
        index = (dz - 1) * 3 + d - 1
        if stage == 1:
            ref = wfull.at[zz, px, core, :, my_cols]
            target = (
                jnp.where(core == 0, x_peer(d)[0], y_peer(d)[0]),
                z,
            )
            return remote(ref, ref, w_send.at[1, index], w_recv.at[1, index], target)
        if stage == 2:
            ref = wfull.at[zz, :, 0, :, my_cols]
            return remote(ref, ref, w_send.at[2, index], w_recv.at[2, index], y_peer(d))
        ref = wfull.at[zz, px, 1, :, :]
        return remote(ref, ref, w_send.at[2, index], w_recv.at[2, index], x_peer(d))

    def last_copy(dz):
        zz = lax.rem(z + dz, NZ)
        ref = wfull.at[zz, :, core, :, :]
        return remote(
            ref, ref, w_send.at[3, dz], w_recv.at[3, dz], (place * NC + 1 - core, z)
        )

    pairs = [(dz, d) for dz in range(1, NZ) for d in range(1, 4)]

    for way in range(2):
        own_copy(0, way).start()
    for dz in range(1, NZ):
        first_copy(dz).start()
    for way in range(2):
        own_copy(1, way).start()

    heads = cols // HD
    span = chunk + 2 * REACH
    qkv[2 * chunk : span, :] = jnp.zeros((span - 2 * chunk, qkv.shape[1]), jnp.bfloat16)
    load_tokens.wait()
    load_qkv.wait()
    lane_block = lax.broadcasted_iota(jnp.int32, (1, span), 1) // BLK

    def attended_copy(c, pair):
        lanes = pl.ds(pair * 2 * HD, 2 * HD)
        there = pl.ds(pl.multiple_of(z * cols + pair * 2 * HD, 2 * HD), 2 * HD)
        return remote(
            att_out.at[chunk_rows(c), lanes],
            att_in.at[:, there],
            att_send.at[c, pair],
            att_recv.at[z, pair],
            (seq, c),
        )

    def project(c):
        x = whole[chunk_rows(c), :].astype(jnp.float32)
        normed = (plain_norm(x) * ngain_ref[...].reshape(1, -1)).astype(jnp.bfloat16)
        qkv[chunk_rows(c), :] = jnp.dot(
            normed, wqkv[...], preferred_element_type=jnp.float32
        ).astype(jnp.bfloat16)

    def attend(c):
        first = pl.multiple_of(jnp.clip(c * chunk - REACH, 0, rows - span), BLK)
        first_block = first // BLK
        key_ids = jnp.zeros((1, span), jnp.int32)
        for b in range(span // BLK):
            key_ids = jnp.where(lane_block == b, ids_ref[0, first_block + b], key_ids)
        same = [
            key_ids == ids_ref[0, c * (chunk // BLK) + b] for b in range(chunk // BLK)
        ]
        for pair in range(heads // 2):
            outputs = []
            for h in range(2):
                base = (2 * pair + h) * 3 * HD
                q = qkv[chunk_rows(c), base : base + HD]
                k = qkv[pl.ds(first, span), base + HD : base + 2 * HD]
                v = qkv[pl.ds(first, span), base + 2 * HD : base + 3 * HD]
                scores = lax.dot_general(
                    q, k, (((1,), (1,)), ((), ())), preferred_element_type=jnp.float32
                )
                probs = []
                for b in range(chunk // BLK):
                    powers = jnp.where(
                        same[b], jnp.exp(scores[b * BLK : (b + 1) * BLK] * HD ** (-0.5)), 0.0
                    )
                    inverse = 1.0 / jnp.sum(powers, axis=-1, keepdims=True)
                    probs.append((powers * inverse).astype(jnp.bfloat16))
                outputs.append(
                    jnp.dot(
                        jnp.concatenate(probs, axis=0), v, preferred_element_type=jnp.float32
                    ).astype(jnp.bfloat16)
                )
            both = jnp.concatenate(outputs, axis=1)

            @pl.when(c == z)
            def _():
                lanes = pl.ds(pl.multiple_of(z * cols + pair * 2 * HD, 2 * HD), 2 * HD)
                att_in[:, lanes] = both

            @pl.when(c != z)
            def _():
                att_out[chunk_rows(c), pair * 2 * HD : (pair + 1) * 2 * HD] = both
                attended_copy(c, pair).start()

    @pl.loop(0, CHUNKS + LAG)
    def _(c):
        @pl.when(c < CHUNKS)
        def _():
            for way in range(2):
                own_copy(c, way).wait_recv()
            for way in range(2):
                forward_copy(c, way).start()

            @pl.when(c + 2 < CHUNKS)
            def _():
                for way in range(2):
                    own_copy(c + 2, way).start()

        @pl.when(c == 0)
        def _():
            for dz in range(1, NZ):
                first_copy(dz).wait_recv()
            for dz, d in pairs:
                plane_copy(1, dz, d).start()

        @pl.when(c == 1)
        def _():
            for dz, d in pairs:
                plane_copy(1, dz, d).wait_recv()

            @pl.when(core == 0)
            def _():
                for dz, d in pairs:
                    plane_copy(2, dz, d).start()

            @pl.when(core == 1)
            def _():
                for dz, d in pairs:
                    plane_copy(3, dz, d).start()

        @pl.when(c >= LAG)
        def _():
            attend(c - LAG)

        @pl.when(c < CHUNKS)
        def _():
            for way in range(2):
                forward_copy(c, way).wait_recv()
            project(c)

        @pl.when(c == CHUNKS - 1)
        def _():
            @pl.when(core == 0)
            def _():
                for dz, d in pairs:
                    plane_copy(2, dz, d).wait_recv()

            @pl.when(core == 1)
            def _():
                for dz, d in pairs:
                    plane_copy(3, dz, d).wait_recv()

            for dz in range(1, NZ):
                last_copy(dz).start()

    load_out.wait()
    for copy in late:
        copy.wait()
    for dz in range(1, NZ):
        last_copy(dz).wait_recv()
    for dz in range(1, NZ):
        source = lax.rem(z + dz, NZ)
        for pair in range(heads // 2):
            lanes = pl.ds(pl.multiple_of(source * cols + pair * 2 * HD, 2 * HD), 2 * HD)
            remote(
                att_in.at[:, lanes], att_in.at[:, lanes], att_send.at[source, pair],
                att_recv.at[source, pair], (seq, source),
            ).wait_recv()

    projected = jnp.dot(
        att_in[...],
        wfull[...].reshape(wfull.shape[4], wfull.shape[4]),
        preferred_element_type=jnp.float32,
    )
    mixed = (whole[chunk_rows(z), :].astype(jnp.float32) + projected).astype(jnp.bfloat16)
    mixed_ref[...] = mixed
    slot_in = (plain_norm(mixed.astype(jnp.float32)) * sgain_ref[...].reshape(1, -1)).astype(jnp.bfloat16)
    keys_buf[...] = jnp.dot(slot_in, wk_ref[...], preferred_element_type=jnp.float32).astype(
        jnp.bfloat16
    )
    values_buf[...] = jnp.dot(slot_in, wv_ref[...], preferred_element_type=jnp.float32).astype(
        jnp.bfloat16
    )

    state = init_ref[pl.ds(start, own), :]
    sent = []
    for it in range(ITERS):
        logits = lax.dot_general(
            query, keys_buf[...], (((1,), (1,)), ((), ())), preferred_element_type=jnp.float32
        ) * width ** (-0.5)
        powers = jnp.exp(logits)
        weights = powers / jnp.sum(powers, axis=0, keepdims=True)
        part[it, :, :width] = jnp.dot(
            weights.astype(jnp.bfloat16), values_buf[...], preferred_element_type=jnp.float32
        )
        denom = jnp.sum(weights, axis=1, keepdims=True)
        part[it, :, width:] = jnp.broadcast_to(denom, (denom.shape[0], 128))

        copies = []
        for step in range(1, NG):
            peer, target = group_peer(step)
            copies.append(
                remote(
                    part.at[it, pl.ds(pl.multiple_of(peer * own, own), own), :],
                    rs_buf.at[it, step],
                    rs_send.at[it, step],
                    rs_recv.at[it, step],
                    target,
                )
            )
        for copy in copies:
            copy.start()
        sent += copies
        from_state = jnp.dot(state, wh_ref[...], precision=HIGH, preferred_element_type=jnp.float32)
        total = part[it, pl.ds(start, own), :]
        for copy in copies:
            copy.wait_recv()
        for step in range(1, NG):
            total = total + rs_buf[it, step]

        ar_buf[it, place] = total
        copies = [
            remote(
                ar_buf.at[it, place],
                ar_buf.at[it, place],
                ar_send.at[it, step],
                ar_recv.at[it, step],
                plane_peer(step)[1],
            )
            for step in range(1, NP)
        ]
        for copy in copies:
            copy.start()
        sent += copies
        for copy in copies:
            copy.wait_recv()
        total = ar_buf[it, 0]
        for peer in range(1, NP):
            total = total + ar_buf[it, peer]

        update = total[:, :width] / total[:, width : width + 1]
        from_in = jnp.dot(update, wi_ref[...], precision=HIGH, preferred_element_type=jnp.float32)
        reset = jax.nn.sigmoid(from_in[:, :width] + from_state[:, :width])
        gate = jax.nn.sigmoid(
            from_in[:, width : 2 * width] + from_state[:, width : 2 * width]
        )
        candidate = jnp.tanh(from_in[:, 2 * width :] + reset * from_state[:, 2 * width :])
        state = (1.0 - gate) * candidate + gate * state
        if it < ITERS - 1:
            message = jnp.dot(
                plain_norm(state), wq_ref[...], precision=HIGH, preferred_element_type=jnp.float32
            )
        else:
            message = state
        ag_buf[it, pl.ds(start, own), :] = message
        copies = [
            remote(
                ag_buf.at[it, pl.ds(start, own), :],
                ag_buf.at[it, pl.ds(start, own), :],
                ag_send.at[it, step],
                ag_recv.at[it, step],
                group_peer(step)[1],
            )
            for step in range(1, NG)
        ]
        for copy in copies:
            copy.start()
        sent += copies
        for copy in copies:
            copy.wait_recv()
        if it < ITERS - 1:
            query = ag_buf[it].astype(jnp.bfloat16)
        else:
            slots_ref[...] = ag_buf[it]

    for copy in sent:
        copy.wait_send()

    @pl.loop(0, CHUNKS)
    def _(c):
        for way in range(2):
            own_copy(c, way).wait_send()
            forward_copy(c, way).wait_send()

        @pl.when(c != z)
        def _():
            for pair in range(heads // 2):
                attended_copy(c, pair).wait_send()

    for dz in range(1, NZ):
        first_copy(dz).wait_send()
        last_copy(dz).wait_send()
    for dz, d in pairs:
        plane_copy(1, dz, d).wait_send()

    @pl.when(core == 0)
    def _():
        for dz, d in pairs:
            plane_copy(2, dz, d).wait_send()

    @pl.when(core == 1)
    def _():
        for dz, d in pairs:
            plane_copy(3, dz, d).wait_send()


def finish_kernel(mixed_ref, slots_ref, mixed_out, slots_out):
    mixed_out[...] = mixed_ref[...]
    slots_out[...] = slots_ref[...]


def local(
    tokens,
    norm_gain,
    w_qkv,
    w_out,
    frame_ids,
    slot_gain,
    w_key,
    w_value,
    w_query,
    slot_init,
    w_input,
    w_hidden,
):
    rows, cols = tokens.shape
    full = cols * NZ
    slots, width = slot_init.shape
    own = slots // NG
    chunk = rows // CHUNKS
    vmem = pl.BlockSpec(memory_space=pltpu.VMEM)
    hbm = pl.BlockSpec(memory_space=pl.ANY)
    share = cols // (NX * NC)
    dma = pltpu.SemaphoreType.DMA
    results = pl.pallas_call(
        block_kernel,
        out_shape=(
            jax.ShapeDtypeStruct((chunk, full), jnp.bfloat16),
            jax.ShapeDtypeStruct((slots, width), jnp.float32),
        ),
        in_specs=[hbm] * 7 + [pl.BlockSpec(memory_space=pltpu.SMEM)] + [vmem] * 4,
        out_specs=(vmem, vmem),
        scratch_shapes=[
            pltpu.VMEM((rows, full), jnp.bfloat16),
            pltpu.VMEM(w_qkv.shape, jnp.bfloat16),
            pltpu.VMEM((NZ, NX, NC, share, full), jnp.bfloat16),
            pltpu.VMEM((rows, w_qkv.shape[1]), jnp.bfloat16),
            pltpu.VMEM((rows, cols), jnp.bfloat16),
            pltpu.VMEM((chunk, full), jnp.bfloat16),
            pltpu.VMEM((chunk, width), jnp.bfloat16),
            pltpu.VMEM((chunk, width), jnp.bfloat16),
            pltpu.VMEM((ITERS, slots, width + 128), jnp.float32),
            pltpu.VMEM((ITERS, NG, own, width + 128), jnp.float32),
            pltpu.VMEM((ITERS, NP, own, width + 128), jnp.float32),
            pltpu.VMEM((ITERS, slots, width), jnp.float32),
            pltpu.VMEM(w_key.shape, jnp.bfloat16),
            pltpu.VMEM(w_value.shape, jnp.bfloat16),
            pltpu.VMEM(w_input.shape, jnp.float32),
            pltpu.VMEM(w_hidden.shape, jnp.float32),
            dma((7,)),
            dma((1,)),
            dma((4, CHUNKS)),
            dma((4, CHUNKS)),
            dma((CHUNKS, 3)),
            dma((NZ, 3)),
            dma((4, 9)),
            dma((4, 9)),
            dma((ITERS, NG)),
            dma((ITERS, NG)),
            dma((ITERS, NP)),
            dma((ITERS, NP)),
            dma((ITERS, NG)),
            dma((ITERS, NG)),
        ],
        compiler_params=pltpu.CompilerParams(
            collective_id=0, has_side_effects=True, vmem_limit_bytes=60 * 1024 * 1024
        ),
        name="vision_block",
    )(
        tokens,
        w_qkv,
        w_out.reshape(NX, NC, share, full),
        w_key,
        w_value,
        w_input,
        w_hidden,
        frame_ids,
        norm_gain,
        slot_gain,
        slot_init,
        w_query,
    )
    return pl.pallas_call(
        finish_kernel,
        out_shape=tuple(jax.ShapeDtypeStruct(r.shape, r.dtype) for r in results),
        in_specs=[vmem] * 2,
        out_specs=(vmem,) * 2,
        name="finish",
    )(*results)


def solution(mesh):
    placed = (
        P("seq", "head"),
        P(),
        P(None, "head"),
        P("head", None),
        P("seq", None),
        P(),
        P(),
        P(),
        P(),
        P(),
        P(),
        P(),
    )
    return jax.shard_map(
        local,
        mesh=mesh,
        in_specs=placed,
        out_specs=(P(("seq", "head"), None), P()),
        check_vma=False,
    )
```

```python
import functools

import jax
import jax.numpy as jnp
from jax import lax
from jax.experimental import pallas as pl
from jax.experimental.pallas import tpu as pltpu
from jax.sharding import PartitionSpec as P

HD = 64
ITERS = 3
BLK = 64
NX, NY, NC, NZ = 4, 4, 2, 4
NG = NZ * NC
NP = NX * NY
CHUNKS = 4
REACH = 3 * BLK
LAG = 2
HIGH = lax.Precision.HIGHEST
MESH = pl.DeviceIdType.MESH


def plain_norm(values):
    mean = jnp.mean(values, axis=-1, keepdims=True)
    centred = values - mean
    var = jnp.mean(centred * centred, axis=-1, keepdims=True)
    return centred * lax.rsqrt(var + 1e-06)


def block_kernel(
    tokens_ref, wqkv_ref, wout_ref, wk_hbm, wv_hbm, wi_hbm, wh_hbm, ids_ref, ngain_ref,
    sgain_ref, init_ref, wq_ref, mixed_ref, slots_ref,
    whole, wqkv, wfull, qkv, att_out, att_in, keys_buf, values_buf,
    relay, part, rs_buf, ar_buf, ag_buf, wk_ref, wv_ref, wi_ref, wh_ref,
    load_sem, own_sem, tok_send, tok_recv, att_send, att_recv, w_send, w_recv,
    half_send, half_recv, last_send, last_recv, rs_send, rs_recv, ar_send, ar_recv, ag_send, ag_recv,
):
    z = lax.axis_index("head")
    seq = lax.axis_index("seq")
    core = lax.rem(seq, NC)
    place = lax.div(seq, NC)
    px, py = lax.div(place, NY), lax.rem(place, NY)
    group = z * NC + core
    rows, cols = tokens_ref.shape
    width = init_ref.shape[1]
    own = init_ref.shape[0] // NG
    chunk = rows // CHUNKS
    half = chunk // 2
    right, left = lax.rem(z + 1, NZ), lax.rem(z + NZ - 1, NZ)

    def device(x, y, c, zz):
        return ((x * NY + y) * NC + c, zz)

    def group_peer(step):
        peer = lax.rem(group + step, NG)
        return peer, (place * NC + lax.rem(peer, NC), lax.div(peer, NC))

    def plane_peer(step):
        peer = lax.rem(place + step, NP)
        return peer, (peer * NC + core, z)

    def remote(src, dst, send, recv, target):
        return pltpu.make_async_remote_copy(
            src_ref=src, dst_ref=dst, send_sem=send, recv_sem=recv,
            device_id=target, device_id_type=MESH,
        )

    barrier = pltpu.get_barrier_semaphore()
    for step in range(1, NG):
        pl.semaphore_signal(barrier, inc=1, device_id=group_peer(step)[1], device_id_type=MESH)
    for step in range(1, NP):
        pl.semaphore_signal(barrier, inc=1, device_id=plane_peer(step)[1], device_id_type=MESH)

    def col(zz):
        return pl.ds(pl.multiple_of(zz * cols, cols), cols)

    load_tokens = pltpu.make_async_copy(tokens_ref, whole.at[:, col(z)], load_sem.at[0])
    load_qkv = pltpu.make_async_copy(wqkv_ref, wqkv, load_sem.at[1])
    load_out = pltpu.make_async_copy(wout_ref, wfull.at[z], load_sem.at[2])
    load_tokens.start()
    load_qkv.start()
    load_out.start()
    late = [
        pltpu.make_async_copy(src, dst, load_sem.at[3 + i])
        for i, (src, dst) in enumerate(
            [(wk_hbm, wk_ref), (wv_hbm, wv_ref), (wi_hbm, wi_ref), (wh_hbm, wh_ref)]
        )
    ]
    for copy in late:
        copy.start()

    start = pl.multiple_of(group * own, own)
    query = jnp.dot(
        plain_norm(init_ref[...]), wq_ref[...], precision=HIGH, preferred_element_type=jnp.float32
    ).astype(jnp.bfloat16)
    pl.semaphore_wait(barrier, NG - 1 + NP - 1)

    def chunk_rows(c):
        return pl.ds(pl.multiple_of(c * chunk, chunk), chunk)

    def own_copy(c, way):
        return remote(
            tokens_ref.at[chunk_rows(c), :],
            whole.at[chunk_rows(c), col(z)],
            tok_send.at[way, c],
            tok_recv.at[way, c],
            (seq, right if way == 0 else left),
        )

    def forward_copy(c, way):
        part_rows = pl.ds(pl.multiple_of(c * chunk + way * half, half), half)
        source = left if way == 0 else right
        return remote(
            whole.at[part_rows, col(source)],
            whole.at[part_rows, col(source)],
            tok_send.at[2 + way, c],
            tok_recv.at[2 + way, c],
            (seq, right if way == 0 else left),
        )

    share = wfull.shape[3]
    wide = wfull.shape[4] // NY
    my_cols = pl.ds(pl.multiple_of(py * wide, wide), wide)

    def first_copy(dz):
        return remote(
            wout_ref.at[px, core, :, my_cols],
            wfull.at[z, px, core, :, my_cols],
            w_send.at[0, dz],
            w_recv.at[0, dz],
            (seq, lax.rem(z + dz, NZ)),
        )

    def x_peer(d):
        return (lax.rem(px + d, NX) * NY + py) * NC + core, z

    def y_peer(d):
        return (px * NY + lax.rem(py + d, NY)) * NC + core, z

    def plane_copy(stage, dz, d):
        zz = lax.rem(z + dz, NZ)
        index = (dz - 1) * 3 + d - 1
        if stage == 1:
            ref = wfull.at[zz, px, core, :, my_cols]
            target = (
                jnp.where(core == 0, x_peer(d)[0], y_peer(d)[0]),
                z,
            )
            return remote(ref, ref, w_send.at[1, index], w_recv.at[1, index], target)
        if stage == 2:
            ref = wfull.at[zz, :, 0, :, my_cols]
            return remote(ref, ref, w_send.at[2, index], w_recv.at[2, index], y_peer(d))
        ref = wfull.at[zz, px, 1, :, :]
        return remote(ref, ref, w_send.at[2, index], w_recv.at[2, index], x_peer(d))

    def last_copy(dz):
        zz = lax.rem(z + dz, NZ)
        ref = wfull.at[zz, :, core, :, :]
        return remote(
            ref, ref, w_send.at[3, dz], w_recv.at[3, dz], (place * NC + 1 - core, z)
        )

    pairs = [(dz, d) for dz in range(1, NZ) for d in range(1, 4)]

    for way in range(2):
        own_copy(0, way).start()
    for dz in range(1, NZ):
        first_copy(dz).start()
    for way in range(2):
        own_copy(1, way).start()

    def pass_on(c):
        for way in range(2):
            own_copy(c, way).wait_recv()
        for way in range(2):
            forward_copy(c, way).start()

        @pl.when(c + 2 < CHUNKS)
        def _():
            for way in range(2):
                own_copy(c + 2, way).start()

    heads = cols // HD
    span = chunk + 2 * REACH
    qkv[2 * chunk : span, :] = jnp.zeros((span - 2 * chunk, qkv.shape[1]), jnp.bfloat16)
    load_tokens.wait()
    load_qkv.wait()
    pass_on(0)
    lane_block = lax.broadcasted_iota(jnp.int32, (1, span), 1) // BLK

    def attended_copy(c, pair):
        lanes = pl.ds(pair * 2 * HD, 2 * HD)
        there = pl.ds(pl.multiple_of(z * cols + pair * 2 * HD, 2 * HD), 2 * HD)
        return remote(
            att_out.at[chunk_rows(c), lanes],
            att_in.at[:, there],
            att_send.at[c, pair],
            att_recv.at[z, pair],
            (seq, c),
        )

    def half_copy(c, way, pair):
        lanes = pl.ds(pair * 2 * HD, 2 * HD)
        return remote(
            att_out.at[pl.ds(pl.multiple_of(c * chunk + way * half, half), half), lanes],
            relay.at[way, :, lanes],
            half_send.at[way, pair],
            half_recv.at[way, pair],
            (seq, right if way == 0 else left),
        )

    def relay_copy(way, pair):
        source = left if way == 0 else right
        there = pl.ds(pl.multiple_of(source * cols + pair * 2 * HD, 2 * HD), 2 * HD)
        return remote(
            relay.at[way, :, pl.ds(pair * 2 * HD, 2 * HD)],
            att_in.at[pl.ds(way * half, half), there],
            last_send.at[way, pair],
            last_recv.at[way, pair],
            (seq, right if way == 0 else left),
        )

    def pass_attended(c):
        for way in range(2):

            @pl.when(c == (right if way == 0 else left))
            def _():
                for pair in range(heads // 2):
                    half_copy(c, way, pair).wait_recv()
                    relay_copy(way, pair).start()

    opposite = lax.rem(z + 2, NZ)

    def project(c):
        x = whole[chunk_rows(c), :].astype(jnp.float32)
        normed = (plain_norm(x) * ngain_ref[...].reshape(1, -1)).astype(jnp.bfloat16)
        qkv[chunk_rows(c), :] = jnp.dot(
            normed, wqkv[...], preferred_element_type=jnp.float32
        ).astype(jnp.bfloat16)

    def attend(c):
        first = pl.multiple_of(jnp.clip(c * chunk - REACH, 0, rows - span), BLK)
        first_block = first // BLK
        key_ids = jnp.zeros((1, span), jnp.int32)
        for b in range(span // BLK):
            key_ids = jnp.where(lane_block == b, ids_ref[0, first_block + b], key_ids)
        same = [
            key_ids == ids_ref[0, c * (chunk // BLK) + b] for b in range(chunk // BLK)
        ]
        for pair in range(heads // 2):
            outputs = []
            for h in range(2):
                base = (2 * pair + h) * 3 * HD
                q = qkv[chunk_rows(c), base : base + HD]
                k = qkv[pl.ds(first, span), base + HD : base + 2 * HD]
                v = qkv[pl.ds(first, span), base + 2 * HD : base + 3 * HD]
                scores = lax.dot_general(
                    q, k, (((1,), (1,)), ((), ())), preferred_element_type=jnp.float32
                )
                probs = []
                for b in range(chunk // BLK):
                    powers = jnp.where(
                        same[b], jnp.exp(scores[b * BLK : (b + 1) * BLK] * HD ** (-0.5)), 0.0
                    )
                    inverse = 1.0 / jnp.sum(powers, axis=-1, keepdims=True)
                    probs.append((powers * inverse).astype(jnp.bfloat16))
                outputs.append(
                    jnp.dot(
                        jnp.concatenate(probs, axis=0), v, preferred_element_type=jnp.float32
                    ).astype(jnp.bfloat16)
                )
            both = jnp.concatenate(outputs, axis=1)

            @pl.when(c == z)
            def _():
                lanes = pl.ds(pl.multiple_of(z * cols + pair * 2 * HD, 2 * HD), 2 * HD)
                att_in[:, lanes] = both

            @pl.when(c != z)
            def _():
                att_out[chunk_rows(c), pair * 2 * HD : (pair + 1) * 2 * HD] = both

                @pl.when(c != opposite)
                def _():
                    attended_copy(c, pair).start()

                @pl.when(c == opposite)
                def _():
                    for way in range(2):
                        half_copy(c, way, pair).start()

    @pl.loop(0, CHUNKS + LAG)
    def _(c):
        @pl.when(c < CHUNKS)
        def _():
            @pl.when(c + 1 < CHUNKS)
            def _():
                pass_on(c + 1)

        @pl.when(c == 0)
        def _():
            for dz in range(1, NZ):
                first_copy(dz).wait_recv()
            for dz, d in pairs:
                plane_copy(1, dz, d).start()

        @pl.when(c == 1)
        def _():
            for dz, d in pairs:
                plane_copy(1, dz, d).wait_recv()

            @pl.when(core == 0)
            def _():
                for dz, d in pairs:
                    plane_copy(2, dz, d).start()

            @pl.when(core == 1)
            def _():
                for dz, d in pairs:
                    plane_copy(3, dz, d).start()

        @pl.when(c >= LAG)
        def _():
            attend(c - LAG)

        @pl.when(c > LAG)
        def _():
            pass_attended(c - LAG - 1)

        @pl.when(c < CHUNKS)
        def _():
            for way in range(2):
                forward_copy(c, way).wait_recv()
            project(c)

        @pl.when(c == CHUNKS - 1)
        def _():
            @pl.when(core == 0)
            def _():
                for dz, d in pairs:
                    plane_copy(2, dz, d).wait_recv()

            @pl.when(core == 1)
            def _():
                for dz, d in pairs:
                    plane_copy(3, dz, d).wait_recv()

            for dz in range(1, NZ):
                last_copy(dz).start()

    pass_attended(CHUNKS - 1)
    load_out.wait()
    for copy in late:
        copy.wait()
    for dz in range(1, NZ):
        last_copy(dz).wait_recv()
    for dz in (1, NZ - 1):
        source = lax.rem(z + dz, NZ)
        for pair in range(heads // 2):
            lanes = pl.ds(pl.multiple_of(source * cols + pair * 2 * HD, 2 * HD), 2 * HD)
            remote(
                att_in.at[:, lanes], att_in.at[:, lanes], att_send.at[source, pair],
                att_recv.at[source, pair], (seq, source),
            ).wait_recv()

    for way in range(2):
        for pair in range(heads // 2):
            relay_copy(way, pair).wait_recv()

    projected = jnp.dot(
        att_in[...],
        wfull[...].reshape(wfull.shape[4], wfull.shape[4]),
        preferred_element_type=jnp.float32,
    )
    mixed = (whole[chunk_rows(z), :].astype(jnp.float32) + projected).astype(jnp.bfloat16)
    mixed_ref[...] = mixed
    slot_in = (plain_norm(mixed.astype(jnp.float32)) * sgain_ref[...].reshape(1, -1)).astype(jnp.bfloat16)
    keys_buf[...] = jnp.dot(slot_in, wk_ref[...], preferred_element_type=jnp.float32).astype(
        jnp.bfloat16
    )
    values_buf[...] = jnp.dot(slot_in, wv_ref[...], preferred_element_type=jnp.float32).astype(
        jnp.bfloat16
    )

    state = init_ref[pl.ds(start, own), :]
    sent = []
    for it in range(ITERS):
        logits = lax.dot_general(
            query, keys_buf[...], (((1,), (1,)), ((), ())), preferred_element_type=jnp.float32
        ) * width ** (-0.5)
        powers = jnp.exp(logits)
        weights = powers / jnp.sum(powers, axis=0, keepdims=True)
        part[it, :, :width] = jnp.dot(
            weights.astype(jnp.bfloat16), values_buf[...], preferred_element_type=jnp.float32
        )
        denom = jnp.sum(weights, axis=1, keepdims=True)
        part[it, :, width:] = jnp.broadcast_to(denom, (denom.shape[0], 128))

        copies = []
        for step in range(1, NG):
            peer, target = group_peer(step)
            copies.append(
                remote(
                    part.at[it, pl.ds(pl.multiple_of(peer * own, own), own), :],
                    rs_buf.at[it, step],
                    rs_send.at[it, step],
                    rs_recv.at[it, step],
                    target,
                )
            )
        for copy in copies:
            copy.start()
        sent += copies
        from_state = jnp.dot(state, wh_ref[...], precision=HIGH, preferred_element_type=jnp.float32)
        total = part[it, pl.ds(start, own), :]
        for copy in copies:
            copy.wait_recv()
        for step in range(1, NG):
            total = total + rs_buf[it, step]

        ar_buf[it, place] = total
        copies = [
            remote(
                ar_buf.at[it, place],
                ar_buf.at[it, place],
                ar_send.at[it, step],
                ar_recv.at[it, step],
                plane_peer(step)[1],
            )
            for step in range(1, NP)
        ]
        for copy in copies:
            copy.start()
        sent += copies
        for copy in copies:
            copy.wait_recv()
        total = ar_buf[it, 0]
        for peer in range(1, NP):
            total = total + ar_buf[it, peer]

        update = total[:, :width] / total[:, width : width + 1]
        from_in = jnp.dot(update, wi_ref[...], precision=HIGH, preferred_element_type=jnp.float32)
        reset = jax.nn.sigmoid(from_in[:, :width] + from_state[:, :width])
        gate = jax.nn.sigmoid(
            from_in[:, width : 2 * width] + from_state[:, width : 2 * width]
        )
        candidate = jnp.tanh(from_in[:, 2 * width :] + reset * from_state[:, 2 * width :])
        state = (1.0 - gate) * candidate + gate * state
        if it < ITERS - 1:
            message = jnp.dot(
                plain_norm(state), wq_ref[...], precision=HIGH, preferred_element_type=jnp.float32
            )
        else:
            message = state
        ag_buf[it, pl.ds(start, own), :] = message
        copies = [
            remote(
                ag_buf.at[it, pl.ds(start, own), :],
                ag_buf.at[it, pl.ds(start, own), :],
                ag_send.at[it, step],
                ag_recv.at[it, step],
                group_peer(step)[1],
            )
            for step in range(1, NG)
        ]
        for copy in copies:
            copy.start()
        sent += copies
        for copy in copies:
            copy.wait_recv()
        if it < ITERS - 1:
            query = ag_buf[it].astype(jnp.bfloat16)
        else:
            slots_ref[...] = ag_buf[it]

    for copy in sent:
        copy.wait_send()

    @pl.loop(0, CHUNKS)
    def _(c):
        for way in range(2):
            own_copy(c, way).wait_send()
            forward_copy(c, way).wait_send()

        @pl.when((c != z) & (c != opposite))
        def _():
            for pair in range(heads // 2):
                attended_copy(c, pair).wait_send()

    for way in range(2):
        for pair in range(heads // 2):
            half_copy(opposite, way, pair).wait_send()
            relay_copy(way, pair).wait_send()

    for dz in range(1, NZ):
        first_copy(dz).wait_send()
        last_copy(dz).wait_send()
    for dz, d in pairs:
        plane_copy(1, dz, d).wait_send()

    @pl.when(core == 0)
    def _():
        for dz, d in pairs:
            plane_copy(2, dz, d).wait_send()

    @pl.when(core == 1)
    def _():
        for dz, d in pairs:
            plane_copy(3, dz, d).wait_send()


def finish_kernel(mixed_ref, slots_ref, mixed_out, slots_out):
    mixed_out[...] = mixed_ref[...]
    slots_out[...] = slots_ref[...]


def local(
    tokens,
    norm_gain,
    w_qkv,
    w_out,
    frame_ids,
    slot_gain,
    w_key,
    w_value,
    w_query,
    slot_init,
    w_input,
    w_hidden,
):
    rows, cols = tokens.shape
    full = cols * NZ
    slots, width = slot_init.shape
    own = slots // NG
    chunk = rows // CHUNKS
    vmem = pl.BlockSpec(memory_space=pltpu.VMEM)
    hbm = pl.BlockSpec(memory_space=pl.ANY)
    share = cols // (NX * NC)
    dma = pltpu.SemaphoreType.DMA
    results = pl.pallas_call(
        block_kernel,
        out_shape=(
            jax.ShapeDtypeStruct((chunk, full), jnp.bfloat16),
            jax.ShapeDtypeStruct((slots, width), jnp.float32),
        ),
        in_specs=[hbm] * 7 + [pl.BlockSpec(memory_space=pltpu.SMEM)] + [vmem] * 4,
        out_specs=(vmem, vmem),
        scratch_shapes=[
            pltpu.VMEM((rows, full), jnp.bfloat16),
            pltpu.VMEM(w_qkv.shape, jnp.bfloat16),
            pltpu.VMEM((NZ, NX, NC, share, full), jnp.bfloat16),
            pltpu.VMEM((rows, w_qkv.shape[1]), jnp.bfloat16),
            pltpu.VMEM((rows, cols), jnp.bfloat16),
            pltpu.VMEM((chunk, full), jnp.bfloat16),
            pltpu.VMEM((chunk, width), jnp.bfloat16),
            pltpu.VMEM((chunk, width), jnp.bfloat16),
            pltpu.VMEM((2, chunk // 2, cols), jnp.bfloat16),
            pltpu.VMEM((ITERS, slots, width + 128), jnp.float32),
            pltpu.VMEM((ITERS, NG, own, width + 128), jnp.float32),
            pltpu.VMEM((ITERS, NP, own, width + 128), jnp.float32),
            pltpu.VMEM((ITERS, slots, width), jnp.float32),
            pltpu.VMEM(w_key.shape, jnp.bfloat16),
            pltpu.VMEM(w_value.shape, jnp.bfloat16),
            pltpu.VMEM(w_input.shape, jnp.float32),
            pltpu.VMEM(w_hidden.shape, jnp.float32),
            dma((7,)),
            dma((1,)),
            dma((4, CHUNKS)),
            dma((4, CHUNKS)),
            dma((CHUNKS, 3)),
            dma((NZ, 3)),
            dma((4, 9)),
            dma((4, 9)),
            dma((2, 3)),
            dma((2, 3)),
            dma((2, 3)),
            dma((2, 3)),
            dma((ITERS, NG)),
            dma((ITERS, NG)),
            dma((ITERS, NP)),
            dma((ITERS, NP)),
            dma((ITERS, NG)),
            dma((ITERS, NG)),
        ],
        compiler_params=pltpu.CompilerParams(
            collective_id=0, has_side_effects=True, vmem_limit_bytes=60 * 1024 * 1024
        ),
        name="vision_block",
    )(
        tokens,
        w_qkv,
        w_out.reshape(NX, NC, share, full),
        w_key,
        w_value,
        w_input,
        w_hidden,
        frame_ids,
        norm_gain,
        slot_gain,
        slot_init,
        w_query,
    )
    return pl.pallas_call(
        finish_kernel,
        out_shape=tuple(jax.ShapeDtypeStruct(r.shape, r.dtype) for r in results),
        in_specs=[vmem] * 2,
        out_specs=(vmem,) * 2,
        name="finish",
    )(*results)


def solution(mesh):
    placed = (
        P("seq", "head"),
        P(),
        P(None, "head"),
        P("head", None),
        P("seq", None),
        P(),
        P(),
        P(),
        P(),
        P(),
        P(),
        P(),
    )
    return jax.shard_map(
        local,
        mesh=mesh,
        in_specs=placed,
        out_specs=(P(("seq", "head"), None), P()),
        check_vma=False,
    )
```
